32 devices in a mesh: groups: 2 (over y), expert: 8 (over z, core), hidden: 2 (over x), tok: 1.
Axes of the slice: x: 2, y: 2, z: 4, core: 2. Of those that a mesh axis runs over, the one named last changes fastest.
Arguments:
- out_grad: bfloat16 [2560, 1152], P(('groups', 'expert', 'tok')), parts along dimension 0, may hold values from -2.5 to 2.5
- expert_index: int32 [2560, 2], P(('groups', 'expert', 'tok')), parts along dimension 0, may hold values from 0 to 3, all different within a row; in each aligned block of 160 rows (0 to 159, 160 to 319, ...) at most 100 rows name the same one
- gate_values: float32 [2560, 2], P(('groups', 'expert', 'tok')), parts along dimension 0, may hold values from 0.2 to 1
- dispatched_inputs: bfloat16 [8, 800, 1152], P('expert', ('groups', 'tok')), parts along dimension 1, may hold values from -6 to 6
- w_gate: bfloat16 [8, 1152, 2304], P('expert', None, 'hidden'), may hold values from -0.1875 to 0.1875
- w_up: bfloat16 [8, 1152, 2304], P('expert', None, 'hidden'), may hold values from -0.1875 to 0.1875
- w_down: bfloat16 [8, 2304, 1152], P('expert', 'hidden'), may hold values from -0.09375 to 0.09375
Outputs:
- input_grad: bfloat16 [2560, 1152], P(('groups', 'expert', 'tok'), 'hidden'), parts along dimension 0
- gate_grad: bfloat16 [2560, 2], P(('groups', 'expert', 'tok')), parts along dimension 0
The draws below stay inside these ranges and needn't reach their ends.
There are 2 independent parts, one for each index of `groups`. The reference program is written for one: setup_inputs(seed, part) draws one part's arguments, and reference() takes and returns one part's arrays. A program takes and returns all parts, laid end to end along the dimension named above; an argument that names none is the same for every part. Nothing has to cross between parts.
Inputs may be any that keep to these rules, and one draw needn't show every extreme that they name: `expert_index`: each row names two different experts. In each aligned block of 160 rows (the rows of one device) no expert is named by more than 100 rows, and in some block some expert is named by exactly 100 rows.
All inputs are finite; a program needn't handle non-finite values.
Results may differ from the reference program's by a relative error of at most 0.014.
Values may be sent and summed in bfloat16 or wider, within the bound.
A program may use at most 64 MiB of HBM per device.

```python
import math
import jax
import jax.numpy as jnp
import numpy as np
from jax import lax

D = 1152
FF = 4608
SPLIT = 2
EXPERTS = 4
TOK_DEV = 160
CAP = 100
TOKENS = 1280
N_EXPERT = 8
N_HIDDEN = 2
N_TOK = 1


def levels(key, extent, pieces, low, high):
    loudness, own = 1.0, jax.random.fold_in(key, 6)
    for position, blocks in pieces:
        heights = jnp.exp(jax.random.uniform(jax.random.fold_in(own, position), (blocks,), jnp.float32, low / len(pieces), high / len(pieces)))
        loudness = loudness * jnp.repeat(heights, extent[position] // blocks).reshape([-1 if axis == position else 1 for axis in range(len(extent))])
    return loudness


def shared_out(own_key, own, number, rows, number_of, top, limit, lean):
    ranking = jax.random.permutation(own_key, number_of)
    heavy_load, common = load_shares(number_of, rows * top, limit, lean, True), load_shares(number_of, rows * top, limit, lean, False)
    places = jnp.arange(number_of)

    def named(tallies, turn):
        used = int((tallies > 0).sum())
        fixed = max(1, used // 4)
        moved = fixed + (places - fixed + turn * (used - fixed)) % max(1, number_of - fixed)
        return jnp.zeros((number_of,), jnp.int32).at[ranking[jnp.where(places < fixed, places, moved)]].set(jnp.asarray(tallies, jnp.int32))

    tallies = jnp.where(number % 4 == 0, named(heavy_load, number // 4), named(common, number - number // 4 - 1))
    mixed = jax.random.permutation(jax.random.fold_in(own, 3), number_of)
    source_of, receiver = mixed[0:number_of // 2 * 2:2], mixed[1:number_of // 2 * 2:2]
    room = jnp.minimum(tallies[source_of] - 1, limit - tallies[receiver]) // 2
    room = jnp.where((source_of == ranking[0]) | (receiver == ranking[0]) | (tallies[receiver] == 0), 0, jnp.maximum(room, 0))
    moved = jax.random.randint(jax.random.fold_in(own, 4), (number_of // 2,), 0, 1 << 20) % (room + 1)
    tallies = tallies.at[source_of].add(-moved).at[receiver].add(moved)
    members = jnp.searchsorted(jnp.cumsum(tallies), jnp.arange(rows * top), side="right").astype(jnp.int32)
    grid = members.reshape(top, rows).T
    grid = grid[jax.random.permutation(jax.random.fold_in(own, 1), rows)]
    turn = jax.random.randint(jax.random.fold_in(own, 2), (rows, 1), 0, top)
    return jnp.take_along_axis(grid, (jnp.arange(top)[None, :] + turn) % top, axis=1)


def load_shares(amount, total, limit, skew, full):
    portions = [(1 << 20) // math.isqrt(standing ** skew) + 1 for standing in range(1, amount + 1)]
    largest = limit if full else min(limit, max(-(-total // amount), total * portions[0] // sum(portions)))
    least = 1 if total - largest >= amount - 1 else 0
    holding, spare = [largest] + [least] * (amount - 1), total - largest - least * (amount - 1)
    while spare > 0:
        candidates = [i for i in range(1, amount) if holding[i] < largest] or [i for i in range(1, amount) if holding[i] < limit]
        pool, budget = sum([portions[i] for i in candidates]), spare
        for i in candidates:
            addition = min(limit - holding[i], max(1, budget * portions[i] // pool), spare)
            holding[i] = holding[i] + addition
            spare = spare - addition
    return np.array(holding)


def bell_draw(own_key, shape, width, reach, split=(), kind=jnp.bfloat16):
    entries = jax.random.normal(own_key, shape, jnp.float32) * width
    if len(split) > 0:
        entries = levels(own_key, shape, split, -0.22, 0.18) * entries
    return jnp.clip(entries, min=-reach, max=reach).astype(kind)


def setup_inputs(seed: int = 0, part: int = 0) -> dict:
    key_list = jax.random.split(jax.random.key(seed), 8)
    part_splits = jax.random.split(jax.random.fold_in(key_list[7], part), 8)
    out_grad = bell_draw(part_splits[0], (TOKENS, D), 0.25, 2.5, ((0, 8),))
    expert_index_keys = jax.random.split(jax.random.fold_in(part_splits[1], 1), TOKENS // TOK_DEV)
    expert_index_turns = jax.random.permutation(jax.random.fold_in(part_splits[1], 3), TOKENS // TOK_DEV)
    expert_index = jax.vmap(lambda own, number: shared_out(jax.random.fold_in(part_splits[1], 2), own, number, TOK_DEV, EXPERTS, 2, CAP, 2))(expert_index_keys, expert_index_turns).reshape((TOKENS, 2))
    gate_values = jnp.clip(0.2 + 0.8 * jax.random.uniform(part_splits[2], (TOKENS, 2), jnp.float32) ** levels(part_splits[2], (TOKENS, 2), ((0, 8),), -0.2, 0.2), 0.2, 1.0)
    dispatched_inputs = bell_draw(part_splits[3], (N_EXPERT, N_TOK * N_EXPERT * CAP // SPLIT, D), 1.0, 6.0, ((0, 8),))
    w_gate = bell_draw(key_list[4], (N_EXPERT, D, FF // SPLIT), D ** -0.5, 0.1875, ((0, 8), (2, 2)))
    w_up = bell_draw(key_list[5], (N_EXPERT, D, FF // SPLIT), D ** -0.5, 0.1875, ((0, 8), (2, 2)))
    w_down = bell_draw(key_list[6], (N_EXPERT, FF // SPLIT, D), FF ** -0.5, 0.09375, ((0, 8), (1, 2)))
    return dict(out_grad=out_grad, expert_index=expert_index, gate_values=gate_values, dispatched_inputs=dispatched_inputs, w_gate=w_gate, w_up=w_up, w_down=w_down)


def slots_of(index_block):
    flat_expert = index_block.reshape(-1)
    onehot = (flat_expert[:, None] == jnp.arange(EXPERTS, dtype=jnp.int32)[None, :]).astype(jnp.int32)
    before = jnp.cumsum(onehot, axis=0) - onehot
    return jnp.sum(onehot * before, axis=1).astype(jnp.int32)


def one_expert(operands):
    inputs, cotangent, gate_mat, up_mat, down_mat = operands
    slot_count = inputs.shape[0]
    group_total = SPLIT * N_HIDDEN
    group_units = FF // group_total
    gate_pre = jnp.dot(inputs, gate_mat, preferred_element_type=jnp.float32)
    up_pre = jnp.dot(inputs, up_mat, preferred_element_type=jnp.float32)
    sigmoid_gate = jax.nn.sigmoid(gate_pre)
    hidden_act = gate_pre * sigmoid_gate * up_pre
    d_hidden = jnp.dot(cotangent, down_mat.T, preferred_element_type=jnp.float32)
    d_up = (d_hidden * gate_pre * sigmoid_gate).astype(jnp.bfloat16)
    d_gate = (d_hidden * up_pre * sigmoid_gate * (1.0 + gate_pre * (1.0 - sigmoid_gate))).astype(jnp.bfloat16)
    gate_terms = jnp.sum((hidden_act * d_hidden).reshape(slot_count, group_total, group_units), axis=2)
    gate_terms = lax.optimization_barrier(gate_terms.astype(jnp.bfloat16)).astype(jnp.float32)
    slot_gate = jnp.sum(gate_terms, axis=1).astype(jnp.bfloat16)
    back_terms = jnp.einsum("rhf,dhf->hrd",
                            d_gate.astype(jnp.float32).reshape(slot_count, group_total, group_units),
                            gate_mat.astype(jnp.float32).reshape(D, group_total, group_units),
                            precision=lax.Precision.HIGHEST)
    back_terms = back_terms + jnp.einsum("rhf,dhf->hrd",
                                         d_up.astype(jnp.float32).reshape(slot_count, group_total, group_units),
                                         up_mat.astype(jnp.float32).reshape(D, group_total, group_units),
                                         precision=lax.Precision.HIGHEST)
    back_terms = lax.optimization_barrier(back_terms.astype(jnp.bfloat16)).astype(jnp.float32)
    slot_grad = jnp.sum(back_terms, axis=0).astype(jnp.bfloat16)
    return slot_grad, slot_gate


def reference(out_grad, expert_index, gate_values, dispatched_inputs, w_gate, w_up, w_down):
    shard_total = N_EXPERT * N_TOK
    slot_total = N_TOK * N_EXPERT * CAP
    half_rows = N_EXPERT * CAP // SPLIT
    half_units = FF // SPLIT
    gate_full = w_gate.reshape(EXPERTS, SPLIT, D, half_units).transpose(0, 2, 1, 3).reshape(EXPERTS, D, FF)
    up_full = w_up.reshape(EXPERTS, SPLIT, D, half_units).transpose(0, 2, 1, 3).reshape(EXPERTS, D, FF)
    down_full = w_down.reshape(EXPERTS, FF, D)
    expert_inputs = dispatched_inputs.reshape(EXPERTS, SPLIT, N_TOK, half_rows, D)
    expert_inputs = expert_inputs.transpose(0, 2, 1, 3, 4).reshape(EXPERTS, slot_total, D)
    slot = jax.vmap(slots_of)(expert_index.reshape(shard_total, TOK_DEV, 2)).reshape(TOKENS, 2)
    shard_id = jnp.arange(TOKENS, dtype=jnp.int32) // TOK_DEV
    source_id = shard_id // N_TOK
    tok_id = shard_id % N_TOK
    dest_row = (expert_index * slot_total + tok_id[:, None] * (N_EXPERT * CAP)
                + source_id[:, None] * CAP + slot).astype(jnp.int32)
    flat_dest = dest_row.reshape(-1)
    routed_grad = jnp.zeros((EXPERTS * slot_total, D), jnp.bfloat16)
    routed_grad = routed_grad.at[flat_dest].set(jnp.repeat(out_grad, 2, axis=0))
    routed_grad = routed_grad.reshape(EXPERTS, slot_total, D)
    slot_grad, slot_gate = lax.map(one_expert, (expert_inputs, routed_grad, gate_full, up_full, down_full))
    picked = slot_grad.reshape(EXPERTS * slot_total, D)[flat_dest].astype(jnp.float32).reshape(TOKENS, 2, D)
    input_grad = jnp.sum(gate_values[:, :, None] * picked, axis=1).astype(jnp.bfloat16)
    gate_grad = slot_gate.reshape(-1)[flat_dest].reshape(TOKENS, 2)
    return input_grad, gate_grad
```

```python
import functools
import jax
import jax.numpy as jnp
from jax import lax
from jax.experimental import pallas as pl
from jax.experimental.pallas import tpu as pltpu
from jax.sharding import PartitionSpec as P

MESH = pl.DeviceIdType.MESH
NT = (((1,), (1,)), ((), ()))


def kernel(
    pairs, capacity, start, capp, sent, saved_rows, share, lanes,
    index_hbm, values_hbm, grad_hbm, own_hbm, gate_hbm, up_hbm, down_hbm,
    out_ref, prod_ref,
    names, values, grad, places, scale_high, scale_low, send,
    w_gate, w_up, w_down, gate_pad, up_pad, saved, routed, act_a, act_b, act_c,
    part, kept, pair_out, pair_in, cross_out, cross_in, home_out, home_in,
    small_sem, weight_sem, own_sem, saved_send, saved_recv, route_send, route_recv,
    near_send, far_send, pair_send, pair_recv, cross_send, cross_recv, home_send, home_recv,
):
    index = lax.axis_index("expert")
    x = lax.axis_index("hidden")
    z = index // 2
    c = index % 2
    half = pairs // 2
    tokens, width = grad.shape
    units = w_gate.shape[1]
    rows_all = start + capp
    used = pl.ds(0, sent)
    mate = {"expert": z * 2 + (1 - c), "hidden": x}
    across = {"expert": index, "hidden": 1 - x}
    primary = x == c

    def chip(place):
        return {"expert": place * 2 + c, "hidden": x}

    def partner(k):
        place, bit = 0, 1
        while bit < pairs:
            place = place + lax.rem(z // bit + k // bit, 2) * bit
            bit *= 2
        return place

    def remote(src, dst, send_sem, recv_sem, device):
        return pltpu.make_async_remote_copy(
            src_ref=src, dst_ref=dst, send_sem=send_sem, recv_sem=recv_sem,
            device_id=device, device_id_type=MESH,
        )

    small = [
        pltpu.make_async_copy(index_hbm, names, small_sem.at[0]),
        pltpu.make_async_copy(grad_hbm, grad, small_sem.at[1]),
        pltpu.make_async_copy(values_hbm, values, small_sem.at[2]),
    ]
    loads = [
        pltpu.make_async_copy(gate_hbm, w_gate, weight_sem.at[0]),
        pltpu.make_async_copy(up_hbm, w_up, weight_sem.at[1]),
        pltpu.make_async_copy(down_hbm, w_down, weight_sem.at[2]),
    ]
    for which, (full, padded) in enumerate(((gate_hbm, gate_pad), (up_hbm, up_pad))):
        for h in range(2):
            loads.append(pltpu.make_async_copy(
                full.at[pl.ds(h * share, share)],
                padded.at[pl.ds(h * lanes, share)],
                weight_sem.at[3 + which * 2 + h],
            ))

    def own_part(m):
        return own_hbm.at[pl.ds(pl.multiple_of(m * saved_rows, 8), saved_rows)]

    def saved_slot(core, m):
        return saved.at[core * half + m, pl.ds(0, saved_rows)]

    def own_load(m):
        return pltpu.make_async_copy(own_part(m), saved_slot(c, m), own_sem.at[m])

    for load in small:
        load.start()

    barrier = pltpu.get_barrier_semaphore()
    pl.semaphore_signal(barrier, inc=1, device_id=mate, device_id_type=MESH)
    pl.semaphore_signal(barrier, inc=1, device_id=across, device_id_type=MESH)
    for k in range(1, pairs):
        pl.semaphore_signal(barrier, inc=1, device_id=chip(partner(k)), device_id_type=MESH)

    if saved_rows < rows_all:
        saved[:, saved_rows:, :] = jnp.zeros((pairs, rows_all - saved_rows, width), jnp.bfloat16)

    if sent < capp:
        routed[:, sent:, :] = jnp.zeros((2 * pairs, capp - sent, width), jnp.bfloat16)
        home_in[:, sent:, :] = jnp.zeros((pairs, capp - sent, lanes), jnp.bfloat16)
    small[0].wait()
    for m in range(half):
        own_load(m).start()
    for load in loads[:2]:
        load.start()
    experts = max(16, pairs)
    first, second = names[0:1, :], names[1:2, :]
    which_expert = lax.broadcasted_iota(jnp.int32, (experts, tokens), 0)
    member = jnp.where((which_expert == first) | (which_expert == second), 1.0, 0.0)
    earlier = jnp.where(
        lax.broadcasted_iota(jnp.int32, (tokens, tokens), 0)
        < lax.broadcasted_iota(jnp.int32, (tokens, tokens), 1), 1.0, 0.0,
    ).astype(jnp.bfloat16)
    counts = jnp.dot(member.astype(jnp.bfloat16), earlier, preferred_element_type=jnp.float32)
    places[...] = (counts + 0.5).astype(jnp.int32) + c * (capacity - start)
    row_at = lax.broadcasted_iota(jnp.int32, (capp, tokens), 0)

    def hit(e, k):
        named = names[k:k + 1, :] == e
        return (row_at == places[e:e + 1, :]) & named

    chosen = jnp.concatenate(
        [jnp.where(hit(e, 0) | hit(e, 1), 1.0, 0.0) for e in range(pairs)], axis=0
    ).astype(jnp.bfloat16)
    small[1].wait()
    send[...] = jnp.dot(chosen, grad[...], preferred_element_type=jnp.float32).astype(
        jnp.bfloat16
    ).reshape(pairs, capp, width)
    routed[index, :sent] = send[z, :sent]

    for load in loads[2:]:
        load.start()
    pl.semaphore_wait(barrier, pairs + 1)

    def away(k):
        place = partner(k)
        return remote(
            send.at[place, used], routed.at[index, used], route_send.at[k], route_recv.at[index], chip(place)
        )

    @pl.when(primary)
    def _():
        if pairs > 2:
            away(pairs - 1).start()

    away(1).start()

    @pl.when(primary)
    def _():
        for k in range(pairs - 2, 1, -1):
            away(k).start()

    def give_saved(m):
        return remote(own_part(m), saved_slot(c, m), saved_send.at[m], saved_recv.at[m], mate)

    def take_saved(m):
        return remote(own_part(m), saved_slot(1 - c, m), saved_send.at[m], saved_recv.at[m], mate)

    for m in range(half):
        give_saved(lax.rem(z + m, half)).start()
    give_route = remote(
        send.at[z, used], routed.at[index, used], route_send.at[0], route_recv.at[index], mate
    )
    give_route.start()

    small[2].wait()
    scales = jnp.concatenate(
        [
            jnp.where(hit(e, 0), values[0:1, :], jnp.where(hit(e, 1), values[1:2, :], 0.0))
            for e in range(pairs)
        ],
        axis=0,
    ).T
    high = scales.astype(jnp.bfloat16)
    scale_high[...] = high
    scale_low[...] = (scales - high.astype(jnp.float32)).astype(jnp.bfloat16)

    for h in range(2):
        for padded in (gate_pad, up_pad):
            padded[pl.ds(h * lanes + share, lanes - share), :] = jnp.zeros(
                (lanes - share, units), jnp.bfloat16
            )

    def near(k):
        block = partner(k) * 2 + c
        return remote(
            routed.at[block, used], routed.at[block, used], near_send.at[k], route_recv.at[block], mate
        )

    def far(k):
        block = partner(k) * 2 + c
        return remote(
            routed.at[block, used], routed.at[block, used], far_send.at[k], route_recv.at[block], across
        )

    def pass_first(k):
        @pl.when(primary)
        def _():
            near(k).wait_recv()
            far(k).start()
            near(k).start()

    def pass_direct(k):
        near(k).wait_recv()
        near(k).start()

    def pass_second(k):
        @pl.when(jnp.logical_not(primary))
        def _():
            near(k).wait_recv()
            near(k).start()

    def wait_mate_block(k):
        block = partner(k) * 2 + (1 - c)
        remote(
            routed.at[block, used], routed.at[block, used], near_send.at[0], route_recv.at[block], mate
        ).wait_recv()

    def forward(place):
        rows = saved[place]
        gate_pre = jnp.dot(rows, w_gate[...], preferred_element_type=jnp.float32)
        up_pre = jnp.dot(rows, w_up[...], preferred_element_type=jnp.float32)
        sig = 0.5 * jnp.tanh(0.5 * gate_pre) + 0.5
        silu = gate_pre * sig
        act_a[place] = silu
        act_b[place] = up_pre * sig * (1.0 + gate_pre * (1.0 - sig))
        act_c[place] = silu * up_pre

    def backward(k, between):
        place = partner(k)
        low, high = routed[place * 2], routed[place * 2 + 1]
        rows = jnp.concatenate(
            [low[:start], low[start:] + high[:capp - start], high[capp - start:]], axis=0
        )
        d_hidden = lax.dot_general(rows, w_down[...], NT, preferred_element_type=jnp.float32)
        d_up = (d_hidden * act_a[place]).astype(jnp.bfloat16)
        d_gate = (d_hidden * act_b[place]).astype(jnp.bfloat16)
        product = jnp.sum(d_hidden * act_c[place], axis=1, keepdims=True)
        between()
        back = lax.dot_general(d_gate, gate_pad[...], NT, preferred_element_type=jnp.float32)
        back = back + lax.dot_general(d_up, up_pad[...], NT, preferred_element_type=jnp.float32)
        for core in range(2):
            block = slice(core * start, core * start + capp)
            for h in range(2):
                part[core, h] = back[block, h * lanes:(h + 1) * lanes]
                part[core, h, :, share:] = jnp.broadcast_to(
                    product[block], (capp, lanes - share)
                )

    def pair_copy(k):
        return remote(pair_out.at[k, :, used], pair_in.at[k, :, used], pair_send.at[k], pair_recv.at[k], mate)

    def cross_copy(k):
        return remote(cross_out.at[k, used], cross_in.at[k, used], cross_send.at[k], cross_recv.at[k], across)

    def home_copy(k):
        return remote(
            home_out.at[k, used], home_in.at[z, used], home_send.at[k], home_recv.at[z], chip(partner(k))
        )

    def pair_start(k):
        pair_out[k] = part[1 - c].astype(jnp.bfloat16)
        pair_copy(k).start()

    def cross_start(k):
        pair_copy(k).wait_recv()
        cross_out[k] = (part[c, 1 - x] + pair_in[k, 1 - x].astype(jnp.float32)).astype(
            jnp.bfloat16
        )
        cross_copy(k).start()
        kept[k] = part[c, x] + pair_in[k, x].astype(jnp.float32)

    def reduced(k):
        cross_copy(k).wait_recv()
        return (kept[k] + cross_in[k].astype(jnp.float32)).astype(jnp.bfloat16)

    def home_start(k):
        home_out[k] = reduced(k)
        home_copy(k).start()

    def own_home():
        home_in[z, :sent] = reduced(0)[:sent]

    def turn(t):
        return jnp.where(t <= 1, t, pairs + 1 - t)

    def ready(place):
        m = lax.rem(place, half)

        @pl.when(place // half == c)
        def _():
            own_load(m).wait()

        @pl.when(place // half != c)
        def _():
            take_saved(m).wait_recv()

    def nothing():
        pass

    loads[0].wait()
    loads[1].wait()
    ready(z)
    forward(z)
    for load in loads[2:]:
        load.wait()
    wait_mate_block(0)
    backward(0, nothing)
    pair_start(0)

    def first_phase(t, carry):
        place = partner(turn(t))
        ready(place)
        forward(place)

        @pl.when(t == 1)
        def _():
            if pairs > 2:
                pass_first(pairs - 1)
            cross_start(0)

        @pl.when(t == min(2, pairs - 1))
        def _():
            pass_direct(1)

        return carry

    lax.fori_loop(1, pairs, first_phase, 0)

    def second_phase(t, carry):
        k = turn(t)
        wait_mate_block(k)

        def between():
            @pl.when(t + 2 < pairs)
            def _():
                pass_first(turn(t + 2))

            @pl.when(t + 1 < pairs)
            def _():
                pass_second(turn(t + 1))

            @pl.when(t >= 2)
            def _():
                cross_start(turn(t - 1))

            @pl.when(t == min(2, pairs - 1))
            def _():
                own_home()

            @pl.when(t >= 3)
            def _():
                home_start(turn(t - 2))

        backward(k, between)
        pair_start(k)
        return carry

    lax.fori_loop(1, pairs, second_phase, 0)
    last = turn(pairs - 1)
    cross_start(last)
    if pairs > 2:
        home_start(turn(pairs - 2))
    home_start(last)

    def arrivals(k, carry):
        place = partner(k)
        remote(
            home_out.at[k, used], home_in.at[place, used], home_send.at[k], home_recv.at[place], chip(place)
        ).wait_recv()
        return carry

    lax.fori_loop(1, pairs, arrivals, 0)

    rows = home_in[...].reshape(pairs * capp, lanes)
    total = jnp.dot(scale_high[...], rows, preferred_element_type=jnp.float32)
    total = total + jnp.dot(scale_low[...], rows, preferred_element_type=jnp.float32)
    out_ref[...] = total[:, :share].astype(jnp.bfloat16)
    for k in range(2):
        gate_row = jnp.zeros((1, tokens), jnp.float32)
        for e in range(pairs):
            column = home_in[e, :, share:share + 1].astype(jnp.float32)
            gate_row = gate_row + jnp.sum(
                jnp.where(hit(e, k), column, 0.0), axis=0, keepdims=True
            )
        prod_ref[k:k + 1, :] = gate_row.astype(jnp.bfloat16)

    for m in range(half):
        give_saved(m).wait_send()
    give_route.wait_send()
    pair_copy(0).wait_send()
    cross_copy(0).wait_send()
    away(1).wait_send()

    def drain(k, carry):
        pair_copy(k).wait_send()
        cross_copy(k).wait_send()
        home_copy(k).wait_send()
        near(k).wait_send()

        @pl.when(primary & (k > 1))
        def _():
            away(k).wait_send()
            far(k).wait_send()

        return carry

    lax.fori_loop(1, pairs, drain, 0)


def local(out_grad, expert_index, gate_values, dispatched_inputs, w_gate, w_up, w_down):
    sources = lax.axis_size("expert")
    pairs = sources // 2
    tokens, width = out_grad.shape
    units = w_gate.shape[2]
    share = width // lax.axis_size("hidden")
    lanes = (share + 128) // 128 * 128
    capacity = 2 * dispatched_inputs.shape[1] // sources
    start = capacity // 16 * 16
    capp = (2 * capacity - start + 15) // 16 * 16
    sent = (2 * capacity - start + 7) // 8 * 8
    rows_all = start + capp
    own = dispatched_inputs[0]
    saved_rows = 2 * capacity
    if saved_rows % 8:
        own = jnp.pad(
            own.reshape(pairs // 2, saved_rows, width),
            ((0, 0), (0, rows_all - saved_rows), (0, 0)),
        ).reshape(-1, width)
        saved_rows = rows_all
    bf16, f32 = jnp.bfloat16, jnp.float32
    vmem = pl.BlockSpec(memory_space=pltpu.VMEM)
    hbm = pl.BlockSpec(memory_space=pl.ANY)
    dma = pltpu.SemaphoreType.DMA
    input_grad, gate_grad = pl.pallas_call(
        functools.partial(kernel, pairs, capacity, start, capp, sent, saved_rows, share, lanes),
        out_shape=(
            jax.ShapeDtypeStruct((tokens, share), bf16),
            jax.ShapeDtypeStruct((2, tokens), bf16),
        ),
        in_specs=[hbm] * 7,
        out_specs=(vmem, vmem),
        scratch_shapes=[
            pltpu.VMEM((2, tokens), jnp.int32),
            pltpu.VMEM((2, tokens), f32),
            pltpu.VMEM((tokens, width), bf16),
            pltpu.VMEM((max(16, pairs), tokens), jnp.int32),
            pltpu.VMEM((tokens, pairs * capp), bf16),
            pltpu.VMEM((tokens, pairs * capp), bf16),
            pltpu.VMEM((pairs, capp, width), bf16),
            pltpu.VMEM((width, units), bf16),
            pltpu.VMEM((width, units), bf16),
            pltpu.VMEM((units, width), bf16),
            pltpu.VMEM((2 * lanes, units), bf16),
            pltpu.VMEM((2 * lanes, units), bf16),
            pltpu.VMEM((pairs, rows_all, width), bf16),
            pltpu.VMEM((sources, capp, width), bf16),
            pltpu.VMEM((pairs, rows_all, units), f32),
            pltpu.VMEM((pairs, rows_all, units), f32),
            pltpu.VMEM((pairs, rows_all, units), f32),
            pltpu.VMEM((2, 2, capp, lanes), f32),
            pltpu.VMEM((pairs, capp, lanes), f32),
            pltpu.VMEM((pairs, 2, capp, lanes), bf16),
            pltpu.VMEM((pairs, 2, capp, lanes), bf16),
            pltpu.VMEM((pairs, capp, lanes), bf16),
            pltpu.VMEM((pairs, capp, lanes), bf16),
            pltpu.VMEM((pairs, capp, lanes), bf16),
            pltpu.VMEM((pairs, capp, lanes), bf16),
            dma((3,)),
            dma((7,)),
            dma((pairs // 2,)),
            dma((pairs // 2,)),
            dma((pairs // 2,)),
            dma((pairs,)),
            dma((sources,)),
            dma((pairs,)),
            dma((pairs,)),
            dma((pairs,)),
            dma((pairs,)),
            dma((pairs,)),
            dma((pairs,)),
            dma((pairs,)),
            dma((pairs,)),
        ],
        compiler_params=pltpu.CompilerParams(
            collective_id=0, has_side_effects=True, vmem_limit_bytes=60 * 1024 * 1024
        ),
    )(expert_index.T, gate_values.T, out_grad, own, w_gate[0], w_up[0], w_down[0])
    return input_grad, gate_grad.T


def solution(mesh):
    in_specs = (
        P(("groups", "expert", "tok"), None),
        P(("groups", "expert", "tok"), None),
        P(("groups", "expert", "tok"), None),
        P("expert", ("groups", "tok"), None),
        P("expert", None, "hidden"),
        P("expert", None, "hidden"),
        P("expert", "hidden", None),
    )
    out_specs = (P(("groups", "expert", "tok"), "hidden"), P(("groups", "expert", "tok"), None))
    return jax.shard_map(local, mesh=mesh, in_specs=in_specs, out_specs=out_specs, check_vma=False)
```

```python
import functools
import jax
import jax.numpy as jnp
from jax import lax
from jax.experimental import pallas as pl
from jax.experimental.pallas import tpu as pltpu
from jax.sharding import PartitionSpec as P

MESH = pl.DeviceIdType.MESH
NT = (((1,), (1,)), ((), ()))


def kernel(
    pairs, capacity, start, capp, sent, saved_rows, share, lanes,
    index_hbm, values_hbm, grad_hbm, own_hbm, gate_hbm, up_hbm, down_hbm,
    out_ref, prod_ref,
    names, values, grad, places, scale, total, gate_total, send,
    w_gate, w_up, w_down, gate_pad, up_pad, saved, routed, act_a, act_b, act_c,
    part, kept, pair_out, pair_in, cross_out, cross_in, home_out, home_in,
    small_sem, weight_sem, own_sem, saved_send, saved_recv, route_send, route_recv,
    near_send, far_send, pair_send, pair_recv, cross_send, cross_recv, home_send, home_recv,
):
    index = lax.axis_index("expert")
    x = lax.axis_index("hidden")
    z = index // 2
    c = index % 2
    half = pairs // 2
    tokens, width = grad.shape
    units = w_gate.shape[1]
    rows_all = start + capp
    used = pl.ds(0, sent)
    mate = {"expert": z * 2 + (1 - c), "hidden": x}
    across = {"expert": index, "hidden": 1 - x}
    primary = x == c

    def chip(place):
        return {"expert": place * 2 + c, "hidden": x}

    def partner(k):
        place, bit = 0, 1
        while bit < pairs:
            place = place + lax.rem(z // bit + k // bit, 2) * bit
            bit *= 2
        return place

    def remote(src, dst, send_sem, recv_sem, device):
        return pltpu.make_async_remote_copy(
            src_ref=src, dst_ref=dst, send_sem=send_sem, recv_sem=recv_sem,
            device_id=device, device_id_type=MESH,
        )

    small = [
        pltpu.make_async_copy(index_hbm, names, small_sem.at[0]),
        pltpu.make_async_copy(grad_hbm, grad, small_sem.at[1]),
        pltpu.make_async_copy(values_hbm, values, small_sem.at[2]),
    ]
    loads = [
        pltpu.make_async_copy(gate_hbm, w_gate, weight_sem.at[0]),
        pltpu.make_async_copy(up_hbm, w_up, weight_sem.at[1]),
        pltpu.make_async_copy(down_hbm, w_down, weight_sem.at[2]),
    ]
    for which, (full, padded) in enumerate(((gate_hbm, gate_pad), (up_hbm, up_pad))):
        for h in range(2):
            loads.append(pltpu.make_async_copy(
                full.at[pl.ds(h * share, share)],
                padded.at[pl.ds(h * lanes, share)],
                weight_sem.at[3 + which * 2 + h],
            ))

    def own_part(m):
        return own_hbm.at[pl.ds(pl.multiple_of(m * saved_rows, 8), saved_rows)]

    def saved_slot(core, m):
        return saved.at[core * half + m, pl.ds(0, saved_rows)]

    def own_load(m):
        return pltpu.make_async_copy(own_part(m), saved_slot(c, m), own_sem.at[m])

    for load in small:
        load.start()

    barrier = pltpu.get_barrier_semaphore()
    pl.semaphore_signal(barrier, inc=1, device_id=mate, device_id_type=MESH)
    pl.semaphore_signal(barrier, inc=1, device_id=across, device_id_type=MESH)
    for k in range(1, pairs):
        pl.semaphore_signal(barrier, inc=1, device_id=chip(partner(k)), device_id_type=MESH)

    if saved_rows < rows_all:
        saved[:, saved_rows:, :] = jnp.zeros((pairs, rows_all - saved_rows, width), jnp.bfloat16)

    if sent < capp:
        routed[:, sent:, :] = jnp.zeros((2 * pairs, capp - sent, width), jnp.bfloat16)
        home_in[:, sent:, :] = jnp.zeros((pairs, capp - sent, lanes), jnp.bfloat16)
    small[0].wait()
    for m in range(half):
        own_load(m).start()
    for load in loads[:2]:
        load.start()
    experts = max(16, pairs)
    first, second = names[0:1, :], names[1:2, :]
    which_expert = lax.broadcasted_iota(jnp.int32, (experts, tokens), 0)
    member = jnp.where((which_expert == first) | (which_expert == second), 1.0, 0.0)
    earlier = jnp.where(
        lax.broadcasted_iota(jnp.int32, (tokens, tokens), 0)
        < lax.broadcasted_iota(jnp.int32, (tokens, tokens), 1), 1.0, 0.0,
    ).astype(jnp.bfloat16)
    counts = jnp.dot(member.astype(jnp.bfloat16), earlier, preferred_element_type=jnp.float32)
    places[...] = (counts + 0.5).astype(jnp.int32) + c * (capacity - start)
    row_at = lax.broadcasted_iota(jnp.int32, (capp, tokens), 0)

    def hit(e, k):
        named = names[k:k + 1, :] == e
        return (row_at == places[e:e + 1, :]) & named

    chosen = jnp.concatenate(
        [jnp.where(hit(e, 0) | hit(e, 1), 1.0, 0.0) for e in range(pairs)], axis=0
    ).astype(jnp.bfloat16)
    small[1].wait()
    send[...] = jnp.dot(chosen, grad[...], preferred_element_type=jnp.float32).astype(
        jnp.bfloat16
    ).reshape(pairs, capp, width)
    routed[index, :sent] = send[z, :sent]

    for load in loads[2:]:
        load.start()
    pl.semaphore_wait(barrier, pairs + 1)

    def away(k):
        place = partner(k)
        return remote(
            send.at[place, used], routed.at[index, used], route_send.at[k], route_recv.at[index], chip(place)
        )

    @pl.when(primary)
    def _():
        for k in range(pairs - 1, 1, -1):
            away(k).start()

    @pl.when(jnp.logical_not(primary))
    def _():
        away(1).start()

    def give_saved(m):
        return remote(own_part(m), saved_slot(c, m), saved_send.at[m], saved_recv.at[m], mate)

    def take_saved(m):
        return remote(own_part(m), saved_slot(1 - c, m), saved_send.at[m], saved_recv.at[m], mate)

    for m in range(half):
        give_saved(lax.rem(z + m, half)).start()
    give_route = remote(
        send.at[z, used], routed.at[index, used], route_send.at[0], route_recv.at[index], mate
    )
    give_route.start()

    small[2].wait()
    for e in range(pairs):
        weight = jnp.where(hit(e, 0), values[0:1, :], jnp.where(hit(e, 1), values[1:2, :], 0.0)).T
        high = weight.astype(jnp.bfloat16)
        scale[e, :tokens] = high
        scale[e, tokens:] = (weight - high.astype(jnp.float32)).astype(jnp.bfloat16)

    for h in range(2):
        for padded in (gate_pad, up_pad):
            padded[pl.ds(h * lanes + share, lanes - share), :] = jnp.zeros(
                (lanes - share, units), jnp.bfloat16
            )

    def near(k):
        block = partner(k) * 2 + c
        return remote(
            routed.at[block, used], routed.at[block, used], near_send.at[k], route_recv.at[block], mate
        )

    def far(k):
        block = partner(k) * 2 + c
        return remote(
            routed.at[block, used], routed.at[block, used], far_send.at[k], route_recv.at[block], across
        )

    def pass_first(k):
        @pl.when(primary)
        def _():
            near(k).wait_recv()
            far(k).start()
            near(k).start()

    def pass_direct(k):
        near(k).wait_recv()
        near(k).start()

    def pass_second(k):
        @pl.when(jnp.logical_not(primary))
        def _():
            near(k).wait_recv()
            near(k).start()

    def wait_mate_block(k):
        block = partner(k) * 2 + (1 - c)
        remote(
            routed.at[block, used], routed.at[block, used], near_send.at[0], route_recv.at[block], mate
        ).wait_recv()

    def forward(place):
        rows = saved[place]
        gate_pre = jnp.dot(rows, w_gate[...], preferred_element_type=jnp.float32)
        up_pre = jnp.dot(rows, w_up[...], preferred_element_type=jnp.float32)
        sig = 0.5 * jnp.tanh(0.5 * gate_pre) + 0.5
        silu = gate_pre * sig
        act_a[place] = silu
        act_b[place] = up_pre * sig * (1.0 + gate_pre * (1.0 - sig))
        act_c[place] = silu * up_pre

    def slot(k):
        return 1 if isinstance(k, int) and k == 0 else 0

    def backward(k, between):
        place = partner(k)
        low, high = routed[place * 2], routed[place * 2 + 1]
        rows = jnp.concatenate(
            [low[:start], low[start:] + high[:capp - start], high[capp - start:]], axis=0
        )
        d_hidden = lax.dot_general(rows, w_down[...], NT, preferred_element_type=jnp.float32)
        d_up = (d_hidden * act_a[place]).astype(jnp.bfloat16)
        d_gate = (d_hidden * act_b[place]).astype(jnp.bfloat16)
        product = jnp.sum(d_hidden * act_c[place], axis=1, keepdims=True)
        between()
        back = lax.dot_general(d_gate, gate_pad[...], NT, preferred_element_type=jnp.float32)
        back = back + lax.dot_general(d_up, up_pad[...], NT, preferred_element_type=jnp.float32)
        for core in range(2):
            block = slice(core * start, core * start + capp)
            for h in range(2):
                part[slot(k), core, h] = back[block, h * lanes:(h + 1) * lanes]
                part[slot(k), core, h, :, share:] = jnp.broadcast_to(
                    product[block], (capp, lanes - share)
                )

    def pair_copy(k):
        return remote(pair_out.at[k, :, used], pair_in.at[k, :, used], pair_send.at[k], pair_recv.at[k], mate)

    def cross_copy(k):
        return remote(cross_out.at[k, used], cross_in.at[k, used], cross_send.at[k], cross_recv.at[k], across)

    def home_copy(k):
        return remote(
            home_out.at[k, used], home_in.at[z, used], home_send.at[k], home_recv.at[z], chip(partner(k))
        )

    def pair_start(k):
        pair_out[k] = part[slot(k), 1 - c].astype(jnp.bfloat16)
        pair_copy(k).start()

    def cross_start(k):
        pair_copy(k).wait_recv()
        cross_out[k] = (part[slot(k), c, 1 - x] + pair_in[k, 1 - x].astype(jnp.float32)).astype(
            jnp.bfloat16
        )
        cross_copy(k).start()
        kept[k] = part[slot(k), c, x] + pair_in[k, x].astype(jnp.float32)

    def reduced(k):
        cross_copy(k).wait_recv()
        return (kept[k] + cross_in[k].astype(jnp.float32)).astype(jnp.bfloat16)

    def home_start(k):
        home_out[k] = reduced(k)
        home_copy(k).start()

    def own_home():
        home_in[z, :sent] = reduced(0)[:sent]

    def turn(t):
        return pairs - t

    def steps(body):
        if pairs <= 4:
            for t in range(1, pairs):
                body(t, 0)
        else:
            lax.fori_loop(1, pairs, body, 0)

    def ready(place):
        m = lax.rem(place, half)

        @pl.when(place // half == c)
        def _():
            own_load(m).wait()

        @pl.when(place // half != c)
        def _():
            take_saved(m).wait_recv()

    def nothing():
        pass

    loads[0].wait()
    loads[1].wait()
    ready(z)
    forward(z)
    for load in loads[2:]:
        load.wait()
    wait_mate_block(0)
    backward(0, nothing)
    pair_start(0)

    @pl.when(primary)
    def _():
        away(1).start()

    relayed = pairs > 2

    def first_phase(t, carry):
        place = partner(turn(t))
        ready(place)
        forward(place)

        @pl.when(t == 1)
        def _():
            if relayed:
                pass_first(pairs - 1)

        return carry

    steps(first_phase)

    if relayed:
        @pl.when(jnp.logical_not(primary))
        def _():
            pass_direct(1)

        pass_second(pairs - 1)
        pass_first(pairs - 2)
    else:
        pass_direct(1)

    def second_phase(t, carry):
        k = turn(t)
        wait_mate_block(k)

        backward(k, nothing)
        pair_start(k)

        @pl.when(t + 2 < pairs)
        def _():
            pass_second(turn(t + 1))

        @pl.when(t + 3 < pairs)
        def _():
            pass_first(turn(t + 2))

        @pl.when((t >= 2) & (t + 1 < pairs))
        def _():
            home_start(turn(t - 1))

        cross_start(k)

        @pl.when(t == 1)
        def _():
            cross_start(0)

            @pl.when(primary & relayed)
            def _():
                pass_direct(1)

        return carry

    steps(second_phase)
    own_home()
    if relayed:
        home_start(2)
    home_start(1)

    def gather(place, first):
        rows = home_in[place]
        sums = jnp.dot(scale[place], rows, preferred_element_type=jnp.float32)
        column = rows[:, share:share + 1].astype(jnp.float32)
        gates = jnp.concatenate(
            [
                jnp.sum(
                    jnp.where(
                        (row_at == places[pl.ds(place, 1), :]) & (names[k:k + 1, :] == place), column, 0.0
                    ),
                    axis=0, keepdims=True,
                )
                for k in range(2)
            ],
            axis=0,
        )
        sums = sums[:tokens] + sums[tokens:]
        return (sums, gates) if first else (total[...] + sums, gate_total[...] + gates)

    total[...], gate_total[...] = gather(z, True)

    def arrived(k):
        place = partner(k)
        remote(
            home_out.at[k, used], home_in.at[place, used], home_send.at[k], home_recv.at[place], chip(place)
        ).wait_recv()
        return place

    def add(t, carry):
        total[...], gate_total[...] = gather(arrived(pairs + 1 - t), False)
        return carry

    lax.fori_loop(2, pairs - 1, add, 0)
    if relayed:
        total[...], gate_total[...] = gather(arrived(1), False)
    sums, gates = gather(arrived(2 if relayed else 1), False)
    out_ref[...] = sums[:, :share].astype(jnp.bfloat16)
    prod_ref[...] = gates.astype(jnp.bfloat16)

    for m in range(half):
        give_saved(m).wait_send()
    give_route.wait_send()
    pair_copy(0).wait_send()
    cross_copy(0).wait_send()
    away(1).wait_send()

    def drain(k, carry):
        pair_copy(k).wait_send()
        cross_copy(k).wait_send()
        home_copy(k).wait_send()
        near(k).wait_send()

        @pl.when(primary & (k > 1))
        def _():
            away(k).wait_send()
            far(k).wait_send()

        return carry

    lax.fori_loop(1, pairs, drain, 0)


def local(out_grad, expert_index, gate_values, dispatched_inputs, w_gate, w_up, w_down):
    sources = lax.axis_size("expert")
    pairs = sources // 2
    tokens, width = out_grad.shape
    units = w_gate.shape[2]
    share = width // lax.axis_size("hidden")
    lanes = (share + 128) // 128 * 128
    capacity = 2 * dispatched_inputs.shape[1] // sources
    start = capacity // 16 * 16
    capp = (2 * capacity - start + 15) // 16 * 16
    sent = (2 * capacity - start + 7) // 8 * 8
    rows_all = start + capp
    own = dispatched_inputs[0]
    saved_rows = 2 * capacity
    if saved_rows % 8:
        own = jnp.pad(
            own.reshape(pairs // 2, saved_rows, width),
            ((0, 0), (0, rows_all - saved_rows), (0, 0)),
        ).reshape(-1, width)
        saved_rows = rows_all
    bf16, f32 = jnp.bfloat16, jnp.float32
    vmem = pl.BlockSpec(memory_space=pltpu.VMEM)
    hbm = pl.BlockSpec(memory_space=pl.ANY)
    dma = pltpu.SemaphoreType.DMA
    input_grad, gate_grad = pl.pallas_call(
        functools.partial(kernel, pairs, capacity, start, capp, sent, saved_rows, share, lanes),
        out_shape=(
            pltpu.VMEM((tokens, share), bf16),
            pltpu.VMEM((2, tokens), bf16),
        ),
        in_specs=[hbm] * 7,
        out_specs=(vmem, vmem),
        scratch_shapes=[
            pltpu.VMEM((2, tokens), jnp.int32),
            pltpu.VMEM((2, tokens), f32),
            pltpu.VMEM((tokens, width), bf16),
            pltpu.VMEM((max(16, pairs), tokens), jnp.int32),
            pltpu.VMEM((pairs, 2 * tokens, capp), bf16),
            pltpu.VMEM((tokens, lanes), f32),
            pltpu.VMEM((2, tokens), f32),
            pltpu.VMEM((pairs, capp, width), bf16),
            pltpu.VMEM((width, units), bf16),
            pltpu.VMEM((width, units), bf16),
            pltpu.VMEM((units, width), bf16),
            pltpu.VMEM((2 * lanes, units), bf16),
            pltpu.VMEM((2 * lanes, units), bf16),
            pltpu.VMEM((pairs, rows_all, width), bf16),
            pltpu.VMEM((sources, capp, width), bf16),
            pltpu.VMEM((pairs, rows_all, units), f32),
            pltpu.VMEM((pairs, rows_all, units), f32),
            pltpu.VMEM((pairs, rows_all, units), f32),
            pltpu.VMEM((2, 2, 2, capp, lanes), f32),
            pltpu.VMEM((pairs, capp, lanes), f32),
            pltpu.VMEM((pairs, 2, capp, lanes), bf16),
            pltpu.VMEM((pairs, 2, capp, lanes), bf16),
            pltpu.VMEM((pairs, capp, lanes), bf16),
            pltpu.VMEM((pairs, capp, lanes), bf16),
            pltpu.VMEM((pairs, capp, lanes), bf16),
            pltpu.VMEM((pairs, capp, lanes), bf16),
            dma((3,)),
            dma((7,)),
            dma((pairs // 2,)),
            dma((pairs // 2,)),
            dma((pairs // 2,)),
            dma((pairs,)),
            dma((sources,)),
            dma((pairs,)),
            dma((pairs,)),
            dma((pairs,)),
            dma((pairs,)),
            dma((pairs,)),
            dma((pairs,)),
            dma((pairs,)),
            dma((pairs,)),
        ],
        compiler_params=pltpu.CompilerParams(
            collective_id=0, has_side_effects=True, vmem_limit_bytes=60 * 1024 * 1024
        ),
    )(expert_index.T, gate_values.T, out_grad, own, w_gate[0], w_up[0], w_down[0])
    return input_grad, gate_grad.T


def solution(mesh):
    in_specs = (
        P(("groups", "expert", "tok"), None),
        P(("groups", "expert", "tok"), None),
        P(("groups", "expert", "tok"), None),
        P("expert", ("groups", "tok"), None),
        P("expert", None, "hidden"),
        P("expert", None, "hidden"),
        P("expert", "hidden", None),
    )
    out_specs = (P(("groups", "expert", "tok"), "hidden"), P(("groups", "expert", "tok"), None))
    return jax.shard_map(local, mesh=mesh, in_specs=in_specs, out_specs=out_specs, check_vma=False)
```

```python
import functools
import jax
import jax.numpy as jnp
from jax import lax
from jax.experimental import pallas as pl
from jax.experimental.pallas import tpu as pltpu
from jax.sharding import PartitionSpec as P

MESH = pl.DeviceIdType.MESH
NT = (((1,), (1,)), ((), ()))


def kernel(
    pairs, capacity, start, capp, sent, saved_rows, share, lanes,
    index_hbm, values_hbm, grad_hbm, own_hbm, gate_hbm, up_hbm, down_hbm,
    out_ref, prod_ref,
    names, values, grad, places, scale, total, gate_total, send,
    w_gate, w_up, w_down, gate_pad, up_pad, saved, routed, act_a, act_b, act_c,
    part, kept, pair_out, pair_in, cross_out, cross_in, home_out, home_in,
    small_sem, weight_sem, own_sem, saved_send, saved_recv, route_send, route_recv,
    near_send, far_send, pair_send, pair_recv, cross_send, cross_recv, home_send, home_recv,
):
    index = lax.axis_index("expert")
    x = lax.axis_index("hidden")
    z = index // 2
    c = index % 2
    half = pairs // 2
    tokens, width = grad.shape
    units = w_gate.shape[1]
    rows_all = start + capp
    used = pl.ds(0, sent)
    slabs = share // 128
    fold = pair_out.shape[2] - slabs * sent - 8
    tail = slabs * sent + fold
    mate = {"expert": z * 2 + (1 - c), "hidden": x}
    across = {"expert": index, "hidden": 1 - x}
    primary = x == c

    def chip(place):
        return {"expert": place * 2 + c, "hidden": x}

    def partner(k):
        place, bit = 0, 1
        while bit < pairs:
            place = place + lax.rem(z // bit + k // bit, 2) * bit
            bit *= 2
        return place

    def remote(src, dst, send_sem, recv_sem, device):
        return pltpu.make_async_remote_copy(
            src_ref=src, dst_ref=dst, send_sem=send_sem, recv_sem=recv_sem,
            device_id=device, device_id_type=MESH,
        )

    small = [
        pltpu.make_async_copy(index_hbm, names, small_sem.at[0]),
        pltpu.make_async_copy(grad_hbm, grad, small_sem.at[1]),
        pltpu.make_async_copy(values_hbm, values, small_sem.at[2]),
    ]
    loads = [
        pltpu.make_async_copy(gate_hbm, w_gate, weight_sem.at[0]),
        pltpu.make_async_copy(up_hbm, w_up, weight_sem.at[1]),
        pltpu.make_async_copy(down_hbm, w_down, weight_sem.at[2]),
    ]
    for which, (full, padded) in enumerate(((gate_hbm, gate_pad), (up_hbm, up_pad))):
        for h in range(2):
            loads.append(pltpu.make_async_copy(
                full.at[pl.ds(h * share, share)],
                padded.at[pl.ds(h * lanes, share)],
                weight_sem.at[3 + which * 2 + h],
            ))

    def own_part(m):
        return own_hbm.at[pl.ds(pl.multiple_of(m * saved_rows, 8), saved_rows)]

    def saved_slot(core, m):
        return saved.at[core * half + m, pl.ds(0, saved_rows)]

    def own_load(m):
        return pltpu.make_async_copy(own_part(m), saved_slot(c, m), own_sem.at[m])

    for load in small:
        load.start()

    barrier = pltpu.get_barrier_semaphore()
    pl.semaphore_signal(barrier, inc=1, device_id=mate, device_id_type=MESH)
    pl.semaphore_signal(barrier, inc=1, device_id=across, device_id_type=MESH)
    for k in range(1, pairs):
        pl.semaphore_signal(barrier, inc=1, device_id=chip(partner(k)), device_id_type=MESH)

    if saved_rows < rows_all:
        saved[:, saved_rows:, :] = jnp.zeros((pairs, rows_all - saved_rows, width), jnp.bfloat16)

    if sent < capp:
        routed[:, sent:, :] = jnp.zeros((2 * pairs, capp - sent, width), jnp.bfloat16)
    small[0].wait()
    for m in range(half):
        own_load(m).start()
    for load in loads[:2]:
        load.start()
    experts = max(16, pairs)
    first, second = names[0:1, :], names[1:2, :]
    which_expert = lax.broadcasted_iota(jnp.int32, (experts, tokens), 0)
    member = jnp.where((which_expert == first) | (which_expert == second), 1.0, 0.0)
    earlier = jnp.where(
        lax.broadcasted_iota(jnp.int32, (tokens, tokens), 0)
        < lax.broadcasted_iota(jnp.int32, (tokens, tokens), 1), 1.0, 0.0,
    ).astype(jnp.bfloat16)
    counts = jnp.dot(member.astype(jnp.bfloat16), earlier, preferred_element_type=jnp.float32)
    places[...] = (counts + 0.5).astype(jnp.int32) + c * (capacity - start)
    row_at = lax.broadcasted_iota(jnp.int32, (capp, tokens), 0)

    def hit(e, k):
        named = names[k:k + 1, :] == e
        return (row_at == places[e:e + 1, :]) & named

    chosen = jnp.concatenate(
        [jnp.where(hit(e, 0) | hit(e, 1), 1.0, 0.0) for e in range(pairs)], axis=0
    ).astype(jnp.bfloat16)
    small[1].wait()
    send[...] = jnp.dot(chosen, grad[...], preferred_element_type=jnp.float32).astype(
        jnp.bfloat16
    ).reshape(pairs, capp, width)
    routed[index, :sent] = send[z, :sent]

    for load in loads[2:]:
        load.start()
    pl.semaphore_wait(barrier, pairs + 1)

    def away(k):
        place = partner(k)
        return remote(
            send.at[place, used], routed.at[index, used], route_send.at[k], route_recv.at[index], chip(place)
        )

    @pl.when(primary)
    def _():
        for k in range(pairs - 1, 1, -1):
            away(k).start()

    @pl.when(jnp.logical_not(primary))
    def _():
        away(1).start()

    def give_saved(m):
        return remote(own_part(m), saved_slot(c, m), saved_send.at[m], saved_recv.at[m], mate)

    def take_saved(m):
        return remote(own_part(m), saved_slot(1 - c, m), saved_send.at[m], saved_recv.at[m], mate)

    for m in range(half):
        give_saved(lax.rem(z + m, half)).start()
    give_route = remote(
        send.at[z, used], routed.at[index, used], route_send.at[0], route_recv.at[index], mate
    )
    give_route.start()

    small[2].wait()
    for e in range(pairs):
        weight = jnp.where(hit(e, 0), values[0:1, :], jnp.where(hit(e, 1), values[1:2, :], 0.0))[:sent].T
        high = weight.astype(jnp.bfloat16)
        scale[e, :tokens] = high
        scale[e, tokens:] = (weight - high.astype(jnp.float32)).astype(jnp.bfloat16)

    for h in range(2):
        for padded in (gate_pad, up_pad):
            padded[pl.ds(h * lanes + share, lanes - share), :] = jnp.zeros(
                (lanes - share, units), jnp.bfloat16
            )

    def near(k):
        block = partner(k) * 2 + c
        return remote(
            routed.at[block, used], routed.at[block, used], near_send.at[k], route_recv.at[block], mate
        )

    def far(k):
        block = partner(k) * 2 + c
        return remote(
            routed.at[block, used], routed.at[block, used], far_send.at[k], route_recv.at[block], across
        )

    def pass_first(k):
        @pl.when(primary)
        def _():
            near(k).wait_recv()
            far(k).start()
            near(k).start()

    def pass_direct(k):
        near(k).wait_recv()
        near(k).start()

    def pass_second(k):
        @pl.when(jnp.logical_not(primary))
        def _():
            near(k).wait_recv()
            near(k).start()

    def wait_mate_block(k):
        block = partner(k) * 2 + (1 - c)
        remote(
            routed.at[block, used], routed.at[block, used], near_send.at[0], route_recv.at[block], mate
        ).wait_recv()

    def forward(place):
        rows = saved[place]
        gate_pre = jnp.dot(rows, w_gate[...], preferred_element_type=jnp.float32)
        up_pre = jnp.dot(rows, w_up[...], preferred_element_type=jnp.float32)
        sig = 0.5 * jnp.tanh(0.5 * gate_pre) + 0.5
        silu = gate_pre * sig
        act_a[place] = silu
        act_b[place] = up_pre * sig * (1.0 + gate_pre * (1.0 - sig))
        act_c[place] = silu * up_pre

    def slot(k):
        return 1 if isinstance(k, int) and k == 0 else 0

    def backward(k, between):
        place = partner(k)
        low, high = routed[place * 2], routed[place * 2 + 1]
        rows = jnp.concatenate(
            [low[:start], low[start:] + high[:capp - start], high[capp - start:]], axis=0
        )
        d_hidden = lax.dot_general(rows, w_down[...], NT, preferred_element_type=jnp.float32)
        d_up = (d_hidden * act_a[place]).astype(jnp.bfloat16)
        d_gate = (d_hidden * act_b[place]).astype(jnp.bfloat16)
        product = jnp.sum(d_hidden * act_c[place], axis=1, keepdims=True)
        between()
        back = lax.dot_general(d_gate, gate_pad[...], NT, preferred_element_type=jnp.float32)
        back = back + lax.dot_general(d_up, up_pad[...], NT, preferred_element_type=jnp.float32)
        diagonal = lax.broadcasted_iota(jnp.int32, (sent, 128), 0) == lax.broadcasted_iota(
            jnp.int32, (sent, 128), 1
        )
        for core in range(2):
            block = slice(core * start, core * start + sent)
            gates = jnp.sum(jnp.where(diagonal, product[block], 0.0), axis=0, keepdims=True)
            for h in range(2):
                half_back = back[block, h * lanes:(h + 1) * lanes]
                for j in range(slabs):
                    part[slot(k), core, h, j * sent:(j + 1) * sent] = half_back[:, j * 128:(j + 1) * 128]
                if fold:
                    rest = half_back[:, slabs * 128:]
                    if fold < sent:
                        rest = rest[:fold] + pltpu.roll(rest[sent - fold:], 64, 1)
                    part[slot(k), core, h, slabs * sent:tail] = rest
                part[slot(k), core, h, tail:] = jnp.broadcast_to(gates, (8, 128))

    def pair_copy(k):
        return remote(pair_out.at[k], pair_in.at[k], pair_send.at[k], pair_recv.at[k], mate)

    def cross_copy(k):
        return remote(cross_out.at[k], cross_in.at[k], cross_send.at[k], cross_recv.at[k], across)

    def home_copy(k):
        return remote(
            home_out.at[k], home_in.at[z], home_send.at[k], home_recv.at[z], chip(partner(k))
        )

    def pair_start(k):
        pair_out[k] = part[slot(k), 1 - c].astype(jnp.bfloat16)
        pair_copy(k).start()

    def cross_start(k):
        pair_copy(k).wait_recv()
        cross_out[k] = (part[slot(k), c, 1 - x] + pair_in[k, 1 - x].astype(jnp.float32)).astype(
            jnp.bfloat16
        )
        cross_copy(k).start()
        kept[k] = part[slot(k), c, x] + pair_in[k, x].astype(jnp.float32)

    def reduced(k):
        cross_copy(k).wait_recv()
        return (kept[k] + cross_in[k].astype(jnp.float32)).astype(jnp.bfloat16)

    def home_start(k):
        home_out[k] = reduced(k)
        home_copy(k).start()

    def own_home():
        home_in[z] = reduced(0)

    def turn(t):
        return pairs - t

    def steps(body):
        if pairs <= 4:
            for t in range(1, pairs):
                body(t, 0)
        else:
            lax.fori_loop(1, pairs, body, 0)

    def ready(place):
        m = lax.rem(place, half)

        @pl.when(place // half == c)
        def _():
            own_load(m).wait()

        @pl.when(place // half != c)
        def _():
            take_saved(m).wait_recv()

    def nothing():
        pass

    loads[0].wait()
    loads[1].wait()
    ready(z)
    forward(z)
    for load in loads[2:]:
        load.wait()
    wait_mate_block(0)
    backward(0, nothing)
    pair_start(0)

    @pl.when(primary)
    def _():
        away(1).start()

    relayed = pairs > 2

    def first_phase(t, carry):
        place = partner(turn(t))
        ready(place)
        forward(place)

        @pl.when(t == 1)
        def _():
            if relayed:
                pass_first(pairs - 1)

        return carry

    steps(first_phase)

    if relayed:
        @pl.when(jnp.logical_not(primary))
        def _():
            pass_direct(1)

        pass_second(pairs - 1)
        pass_first(pairs - 2)
    else:
        pass_direct(1)

    def second_phase(t, carry):
        k = turn(t)
        wait_mate_block(k)

        backward(k, nothing)
        pair_start(k)

        @pl.when(t + 2 < pairs)
        def _():
            pass_second(turn(t + 1))

        @pl.when(t + 3 < pairs)
        def _():
            pass_first(turn(t + 2))

        @pl.when((t >= 2) & (t + 1 < pairs))
        def _():
            home_start(turn(t - 1))

        cross_start(k)

        @pl.when(t == 1)
        def _():
            cross_start(0)

            @pl.when(primary & relayed)
            def _():
                pass_direct(1)

        return carry

    steps(second_phase)
    own_home()
    if relayed:
        home_start(2)
    home_start(1)

    def gather(place, first):
        packed = home_in[place]
        columns = [packed[j * sent:(j + 1) * sent] for j in range(slabs)]
        if fold:
            rest = packed[slabs * sent:tail]
            if fold < sent:
                rest = rest.astype(jnp.float32)
                lower = pltpu.roll(rest, 64, 1)[2 * fold - sent:]
                rest = jnp.concatenate([rest, lower], axis=0).astype(jnp.bfloat16)
            columns.append(rest)
        sums = jnp.dot(scale[place], jnp.concatenate(columns, axis=1), preferred_element_type=jnp.float32)
        product = packed[tail:, :sent]
        taken = row_at[:sent] == places[pl.ds(place, 1), :]
        gates = jnp.concatenate(
            [
                jnp.dot(
                    product,
                    jnp.where(taken & (names[k:k + 1, :] == place), 1.0, 0.0).astype(jnp.bfloat16),
                    preferred_element_type=jnp.float32,
                )[:1]
                for k in range(2)
            ],
            axis=0,
        )
        sums = sums[:tokens] + sums[tokens:]
        return (sums, gates) if first else (total[...] + sums, gate_total[...] + gates)

    total[...], gate_total[...] = gather(z, True)

    def arrived(k):
        place = partner(k)
        remote(
            home_out.at[k], home_in.at[place], home_send.at[k], home_recv.at[place], chip(place)
        ).wait_recv()
        return place

    def add(t, carry):
        total[...], gate_total[...] = gather(arrived(pairs + 1 - t), False)
        return carry

    lax.fori_loop(2, pairs - 1, add, 0)
    if relayed:
        total[...], gate_total[...] = gather(arrived(1), False)
    sums, gates = gather(arrived(2 if relayed else 1), False)
    out_ref[...] = sums[:, :share].astype(jnp.bfloat16)
    prod_ref[...] = gates.astype(jnp.bfloat16)

    for m in range(half):
        give_saved(m).wait_send()
    give_route.wait_send()
    pair_copy(0).wait_send()
    cross_copy(0).wait_send()
    away(1).wait_send()

    def drain(k, carry):
        pair_copy(k).wait_send()
        cross_copy(k).wait_send()
        home_copy(k).wait_send()
        near(k).wait_send()

        @pl.when(primary & (k > 1))
        def _():
            away(k).wait_send()
            far(k).wait_send()

        return carry

    lax.fori_loop(1, pairs, drain, 0)


def local(out_grad, expert_index, gate_values, dispatched_inputs, w_gate, w_up, w_down):
    sources = lax.axis_size("expert")
    pairs = sources // 2
    tokens, width = out_grad.shape
    units = w_gate.shape[2]
    share = width // lax.axis_size("hidden")
    lanes = (share + 128) // 128 * 128
    capacity = 2 * dispatched_inputs.shape[1] // sources
    start = capacity // 16 * 16
    capp = (2 * capacity - start + 15) // 16 * 16
    sent = (2 * capacity - start + 7) // 8 * 8
    rows_all = start + capp
    assert sent <= 128
    fold = 0 if share % 128 == 0 else (sent + 15) // 16 * 8 if share % 128 == 64 else sent
    packed = share // 128 * sent + fold + 8
    wide = (share + 127) // 128 * 128
    own = dispatched_inputs[0]
    saved_rows = 2 * capacity
    if saved_rows % 8:
        own = jnp.pad(
            own.reshape(pairs // 2, saved_rows, width),
            ((0, 0), (0, rows_all - saved_rows), (0, 0)),
        ).reshape(-1, width)
        saved_rows = rows_all
    bf16, f32 = jnp.bfloat16, jnp.float32
    vmem = pl.BlockSpec(memory_space=pltpu.VMEM)
    hbm = pl.BlockSpec(memory_space=pl.ANY)
    dma = pltpu.SemaphoreType.DMA
    input_grad, gate_grad = pl.pallas_call(
        functools.partial(kernel, pairs, capacity, start, capp, sent, saved_rows, share, lanes),
        out_shape=(
            pltpu.VMEM((tokens, share), bf16),
            pltpu.VMEM((2, tokens), bf16),
        ),
        in_specs=[hbm] * 7,
        out_specs=(vmem, vmem),
        scratch_shapes=[
            pltpu.VMEM((2, tokens), jnp.int32),
            pltpu.VMEM((2, tokens), f32),
            pltpu.VMEM((tokens, width), bf16),
            pltpu.VMEM((max(16, pairs), tokens), jnp.int32),
            pltpu.VMEM((pairs, 2 * tokens, sent), bf16),
            pltpu.VMEM((tokens, wide), f32),
            pltpu.VMEM((2, tokens), f32),
            pltpu.VMEM((pairs, capp, width), bf16),
            pltpu.VMEM((width, units), bf16),
            pltpu.VMEM((width, units), bf16),
            pltpu.VMEM((units, width), bf16),
            pltpu.VMEM((2 * lanes, units), bf16),
            pltpu.VMEM((2 * lanes, units), bf16),
            pltpu.VMEM((pairs, rows_all, width), bf16),
            pltpu.VMEM((sources, capp, width), bf16),
            pltpu.VMEM((pairs, rows_all, units), f32),
            pltpu.VMEM((pairs, rows_all, units), f32),
            pltpu.VMEM((pairs, rows_all, units), f32),
            pltpu.VMEM((2, 2, 2, packed, 128), f32),
            pltpu.VMEM((pairs, packed, 128), f32),
            pltpu.VMEM((pairs, 2, packed, 128), bf16),
            pltpu.VMEM((pairs, 2, packed, 128), bf16),
            pltpu.VMEM((pairs, packed, 128), bf16),
            pltpu.VMEM((pairs, packed, 128), bf16),
            pltpu.VMEM((pairs, packed, 128), bf16),
            pltpu.VMEM((pairs, packed, 128), bf16),
            dma((3,)),
            dma((7,)),
            dma((pairs // 2,)),
            dma((pairs // 2,)),
            dma((pairs // 2,)),
            dma((pairs,)),
            dma((sources,)),
            dma((pairs,)),
            dma((pairs,)),
            dma((pairs,)),
            dma((pairs,)),
            dma((pairs,)),
            dma((pairs,)),
            dma((pairs,)),
            dma((pairs,)),
        ],
        compiler_params=pltpu.CompilerParams(
            collective_id=0, has_side_effects=True, vmem_limit_bytes=60 * 1024 * 1024
        ),
    )(expert_index.T, gate_values.T, out_grad, own, w_gate[0], w_up[0], w_down[0])
    return input_grad, gate_grad.T


def solution(mesh):
    in_specs = (
        P(("groups", "expert", "tok"), None),
        P(("groups", "expert", "tok"), None),
        P(("groups", "expert", "tok"), None),
        P("expert", ("groups", "tok"), None),
        P("expert", None, "hidden"),
        P("expert", None, "hidden"),
        P("expert", "hidden", None),
    )
    out_specs = (P(("groups", "expert", "tok"), "hidden"), P(("groups", "expert", "tok"), None))
    return jax.shard_map(local, mesh=mesh, in_specs=in_specs, out_specs=out_specs, check_vma=False)
```

```python
import functools
import jax
import jax.numpy as jnp
from jax import lax
from jax.experimental import pallas as pl
from jax.experimental.pallas import tpu as pltpu
from jax.sharding import PartitionSpec as P

MESH = pl.DeviceIdType.MESH
NT = (((1,), (1,)), ((), ()))


def kernel(
    pairs, capacity, start, capp, sent, saved_rows, share, lanes,
    index_hbm, values_hbm, grad_hbm, own_hbm, gate_hbm, up_hbm, down_hbm,
    out_ref, prod_ref,
    names, values, grad, places, scale, total, gate_total, send,
    w_gate, w_up, w_down, gate_pad, up_pad, saved, routed, act_a, act_b, act_c,
    part, kept, pair_out, pair_in, cross_out, cross_in, home_out, home_in,
    small_sem, weight_sem, own_sem, saved_send, saved_recv, route_send, route_recv,
    near_send, far_send, pair_send, pair_recv, cross_send, cross_recv, home_send, home_recv,
):
    index = lax.axis_index("expert")
    x = lax.axis_index("hidden")
    z = index // 2
    c = index % 2
    half = pairs // 2
    tokens, width = grad.shape
    units = w_gate.shape[1]
    rows_all = start + capp
    used = pl.ds(0, sent)
    slabs = share // 128
    fold = pair_out.shape[2] - slabs * sent - 8
    tail = slabs * sent + fold
    mate = {"expert": z * 2 + (1 - c), "hidden": x}
    across = {"expert": index, "hidden": 1 - x}
    primary = x == c

    def chip(place):
        return {"expert": place * 2 + c, "hidden": x}

    def partner(k):
        place, bit = 0, 1
        while bit < pairs:
            place = place + lax.rem(z // bit + k // bit, 2) * bit
            bit *= 2
        return place

    def remote(src, dst, send_sem, recv_sem, device):
        return pltpu.make_async_remote_copy(
            src_ref=src, dst_ref=dst, send_sem=send_sem, recv_sem=recv_sem,
            device_id=device, device_id_type=MESH,
        )

    small = [
        pltpu.make_async_copy(index_hbm, names, small_sem.at[0]),
        pltpu.make_async_copy(grad_hbm, grad, small_sem.at[1]),
        pltpu.make_async_copy(values_hbm, values, small_sem.at[2]),
    ]
    loads = [
        pltpu.make_async_copy(gate_hbm, w_gate, weight_sem.at[0]),
        pltpu.make_async_copy(up_hbm, w_up, weight_sem.at[1]),
        pltpu.make_async_copy(down_hbm, w_down, weight_sem.at[2]),
    ]
    for which, (full, padded) in enumerate(((gate_hbm, gate_pad), (up_hbm, up_pad))):
        for h in range(2):
            loads.append(pltpu.make_async_copy(
                full.at[pl.ds(h * share, share)],
                padded.at[pl.ds(h * lanes, share)],
                weight_sem.at[3 + which * 2 + h],
            ))

    def own_part(m):
        return own_hbm.at[pl.ds(pl.multiple_of(m * saved_rows, 8), saved_rows)]

    def saved_slot(core, m):
        return saved.at[core * half + m, pl.ds(0, saved_rows)]

    def own_load(m):
        return pltpu.make_async_copy(own_part(m), saved_slot(c, m), own_sem.at[m])

    for load in small:
        load.start()

    barrier = pltpu.get_barrier_semaphore()
    pl.semaphore_signal(barrier, inc=1, device_id=mate, device_id_type=MESH)
    pl.semaphore_signal(barrier, inc=1, device_id=across, device_id_type=MESH)
    for k in range(1, pairs):
        pl.semaphore_signal(barrier, inc=1, device_id=chip(partner(k)), device_id_type=MESH)

    if saved_rows < rows_all:
        saved[:, saved_rows:, :] = jnp.zeros((pairs, rows_all - saved_rows, width), jnp.bfloat16)

    if sent < capp:
        routed[:, sent:, :] = jnp.zeros((2 * pairs, capp - sent, width), jnp.bfloat16)
    small[0].wait()
    for m in range(half):
        own_load(m).start()
    for load in loads[:2]:
        load.start()
    experts = max(16, pairs)
    first, second = names[0:1, :], names[1:2, :]
    which_expert = lax.broadcasted_iota(jnp.int32, (experts, tokens), 0)
    member = jnp.where((which_expert == first) | (which_expert == second), 1.0, 0.0)
    earlier = jnp.where(
        lax.broadcasted_iota(jnp.int32, (tokens, tokens), 0)
        < lax.broadcasted_iota(jnp.int32, (tokens, tokens), 1), 1.0, 0.0,
    ).astype(jnp.bfloat16)
    counts = jnp.dot(member.astype(jnp.bfloat16), earlier, preferred_element_type=jnp.float32)
    places[...] = (counts + 0.5).astype(jnp.int32) + c * (capacity - start)
    row_at = lax.broadcasted_iota(jnp.int32, (capp, tokens), 0)

    def hit(e, k):
        named = names[k:k + 1, :] == e
        return (row_at == places[e:e + 1, :]) & named

    chosen = jnp.concatenate(
        [jnp.where(hit(e, 0) | hit(e, 1), 1.0, 0.0) for e in range(pairs)], axis=0
    ).astype(jnp.bfloat16)
    small[1].wait()
    send[...] = jnp.dot(chosen, grad[...], preferred_element_type=jnp.float32).astype(
        jnp.bfloat16
    ).reshape(pairs, capp, width)
    routed[index, :sent] = send[z, :sent]

    for load in loads[2:]:
        load.start()
    pl.semaphore_wait(barrier, pairs + 1)

    def away(k):
        place = partner(k)
        return remote(
            send.at[place, used], routed.at[index, used], route_send.at[k], route_recv.at[index], chip(place)
        )

    @pl.when(primary)
    def _():
        for k in range(pairs - 1, 1, -1):
            away(k).start()

    @pl.when(jnp.logical_not(primary))
    def _():
        away(1).start()

    def give_saved(m):
        return remote(own_part(m), saved_slot(c, m), saved_send.at[m], saved_recv.at[m], mate)

    def take_saved(m):
        return remote(own_part(m), saved_slot(1 - c, m), saved_send.at[m], saved_recv.at[m], mate)

    for m in range(half):
        give_saved(lax.rem(z + m, half)).start()
    give_route = remote(
        send.at[z, used], routed.at[index, used], route_send.at[0], route_recv.at[index], mate
    )
    give_route.start()

    small[2].wait()
    for e in range(pairs):
        weight = jnp.where(hit(e, 0), values[0:1, :], jnp.where(hit(e, 1), values[1:2, :], 0.0))[:sent].T
        high = weight.astype(jnp.bfloat16)
        scale[e, :tokens] = high
        scale[e, tokens:] = (weight - high.astype(jnp.float32)).astype(jnp.bfloat16)

    for h in range(2):
        for padded in (gate_pad, up_pad):
            padded[pl.ds(h * lanes + share, lanes - share), :] = jnp.zeros(
                (lanes - share, units), jnp.bfloat16
            )

    def near(k):
        block = partner(k) * 2 + c
        return remote(
            routed.at[block, used], routed.at[block, used], near_send.at[k], route_recv.at[block], mate
        )

    def far(k):
        block = partner(k) * 2 + c
        return remote(
            routed.at[block, used], routed.at[block, used], far_send.at[k], route_recv.at[block], across
        )

    def pass_first(k):
        @pl.when(primary)
        def _():
            near(k).wait_recv()
            far(k).start()
            near(k).start()

    def pass_direct(k):
        near(k).wait_recv()
        near(k).start()

    def pass_second(k):
        @pl.when(jnp.logical_not(primary))
        def _():
            near(k).wait_recv()
            near(k).start()

    def wait_mate_block(k):
        block = partner(k) * 2 + (1 - c)
        remote(
            routed.at[block, used], routed.at[block, used], near_send.at[0], route_recv.at[block], mate
        ).wait_recv()

    def forward(place):
        rows = saved[place]
        gate_pre = jnp.dot(rows, w_gate[...], preferred_element_type=jnp.float32)
        up_pre = jnp.dot(rows, w_up[...], preferred_element_type=jnp.float32)
        sig = 0.5 * jnp.tanh(0.5 * gate_pre) + 0.5
        silu = gate_pre * sig
        act_a[place] = silu
        act_b[place] = up_pre * sig * (1.0 + gate_pre * (1.0 - sig))
        act_c[place] = silu * up_pre

    def slot(k):
        return 1 if isinstance(k, int) and k == 0 else 0

    def backward(k, between):
        place = partner(k)
        low, high = routed[place * 2], routed[place * 2 + 1]
        rows = jnp.concatenate(
            [low[:start], low[start:] + high[:capp - start], high[capp - start:]], axis=0
        )
        d_hidden = lax.dot_general(rows, w_down[...], NT, preferred_element_type=jnp.float32)
        d_up = (d_hidden * act_a[place]).astype(jnp.bfloat16)
        d_gate = (d_hidden * act_b[place]).astype(jnp.bfloat16)
        product = jnp.sum(d_hidden * act_c[place], axis=1, keepdims=True)
        between()
        back = lax.dot_general(d_gate, gate_pad[...], NT, preferred_element_type=jnp.float32)
        back = back + lax.dot_general(d_up, up_pad[...], NT, preferred_element_type=jnp.float32)
        diagonal = lax.broadcasted_iota(jnp.int32, (sent, 128), 0) == lax.broadcasted_iota(
            jnp.int32, (sent, 128), 1
        )
        for core in range(2):
            block = slice(core * start, core * start + sent)
            gates = jnp.sum(jnp.where(diagonal, product[block], 0.0), axis=0, keepdims=True)
            for h in range(2):
                half_back = back[block, h * lanes:(h + 1) * lanes]
                for j in range(slabs):
                    part[slot(k), core, h, j * sent:(j + 1) * sent] = half_back[:, j * 128:(j + 1) * 128]
                if fold:
                    rest = half_back[:, slabs * 128:]
                    if fold < sent:
                        rest = rest[:fold] + pltpu.roll(rest[sent - fold:], 64, 1)
                    part[slot(k), core, h, slabs * sent:tail] = rest
                part[slot(k), core, h, tail:] = jnp.broadcast_to(gates, (8, 128))

    def pair_copy(k):
        return remote(pair_out.at[k], pair_in.at[k], pair_send.at[k], pair_recv.at[k], mate)

    def cross_copy(k):
        return remote(cross_out.at[k], cross_in.at[k], cross_send.at[k], cross_recv.at[k], across)

    def home_copy(k):
        return remote(
            home_out.at[k], home_in.at[z], home_send.at[k], home_recv.at[z], chip(partner(k))
        )

    def pair_start(k):
        pair_out[k] = part[slot(k), 1 - c].astype(jnp.bfloat16)
        pair_copy(k).start()

    def cross_start(k):
        pair_copy(k).wait_recv()
        cross_out[k] = (part[slot(k), c, 1 - x] + pair_in[k, 1 - x].astype(jnp.float32)).astype(
            jnp.bfloat16
        )
        cross_copy(k).start()
        kept[k] = part[slot(k), c, x] + pair_in[k, x].astype(jnp.float32)

    def reduced(k):
        cross_copy(k).wait_recv()
        return (kept[k] + cross_in[k].astype(jnp.float32)).astype(jnp.bfloat16)

    def home_start(k):
        home_out[k] = reduced(k)
        home_copy(k).start()

    def own_home():
        home_in[z] = reduced(0)

    def turn(t):
        return pairs - t

    def steps(body):
        if pairs <= 4:
            for t in range(1, pairs):
                body(t, 0)
        else:
            lax.fori_loop(1, pairs, body, 0)

    def ready(place):
        m = lax.rem(place, half)

        @pl.when(place // half == c)
        def _():
            own_load(m).wait()

        @pl.when(place // half != c)
        def _():
            take_saved(m).wait_recv()

    def nothing():
        pass

    loads[0].wait()
    loads[1].wait()
    ready(z)
    forward(z)
    for load in loads[2:]:
        load.wait()
    wait_mate_block(0)
    backward(0, nothing)
    pair_start(0)

    @pl.when(primary)
    def _():
        away(1).start()

    relayed = pairs > 2

    def first_phase(t, carry):
        place = partner(turn(t))
        ready(place)
        forward(place)

        @pl.when(t == 1)
        def _():
            if relayed:
                pass_first(pairs - 1)

        return carry

    steps(first_phase)

    if relayed:
        @pl.when(jnp.logical_not(primary))
        def _():
            pass_direct(1)

        pass_second(pairs - 1)
        pass_first(pairs - 2)
    else:
        pass_direct(1)

    def second_phase(t, carry):
        k = turn(t)
        wait_mate_block(k)

        backward(k, nothing)
        pair_start(k)

        @pl.when(t + 2 < pairs)
        def _():
            pass_second(turn(t + 1))

        @pl.when(t + 3 < pairs)
        def _():
            pass_first(turn(t + 2))

        cross_start(k)

        @pl.when((t >= 2) & (t + 1 < pairs))
        def _():
            home_start(turn(t - 1))

        @pl.when(t == 1)
        def _():
            cross_start(0)

            @pl.when(primary & relayed)
            def _():
                pass_direct(1)

        return carry

    steps(second_phase)
    own_home()
    if relayed:
        home_start(2)
    home_start(1)

    def gather(place, first):
        packed = home_in[place]
        columns = [packed[j * sent:(j + 1) * sent] for j in range(slabs)]
        if fold:
            rest = packed[slabs * sent:tail]
            if fold < sent:
                rest = rest.astype(jnp.float32)
                lower = pltpu.roll(rest, 64, 1)[2 * fold - sent:]
                rest = jnp.concatenate([rest, lower], axis=0).astype(jnp.bfloat16)
            columns.append(rest)
        sums = jnp.dot(scale[place], jnp.concatenate(columns, axis=1), preferred_element_type=jnp.float32)
        product = packed[tail:, :sent]
        taken = row_at[:sent] == places[pl.ds(place, 1), :]
        gates = jnp.concatenate(
            [
                jnp.dot(
                    product,
                    jnp.where(taken & (names[k:k + 1, :] == place), 1.0, 0.0).astype(jnp.bfloat16),
                    preferred_element_type=jnp.float32,
                )[:1]
                for k in range(2)
            ],
            axis=0,
        )
        sums = sums[:tokens] + sums[tokens:]
        return (sums, gates) if first else (total[...] + sums, gate_total[...] + gates)

    total[...], gate_total[...] = gather(z, True)

    def arrived(k):
        place = partner(k)
        remote(
            home_out.at[k], home_in.at[place], home_send.at[k], home_recv.at[place], chip(place)
        ).wait_recv()
        return place

    def add(t, carry):
        total[...], gate_total[...] = gather(arrived(pairs + 1 - t), False)
        return carry

    lax.fori_loop(2, pairs - 1, add, 0)
    if relayed:
        total[...], gate_total[...] = gather(arrived(1), False)
    sums, gates = gather(arrived(2 if relayed else 1), False)
    out_ref[...] = sums[:, :share].astype(jnp.bfloat16)
    prod_ref[...] = gates.astype(jnp.bfloat16)

    for m in range(half):
        give_saved(m).wait_send()
    give_route.wait_send()
    pair_copy(0).wait_send()
    cross_copy(0).wait_send()
    away(1).wait_send()

    def drain(k, carry):
        pair_copy(k).wait_send()
        cross_copy(k).wait_send()
        home_copy(k).wait_send()
        near(k).wait_send()

        @pl.when(primary & (k > 1))
        def _():
            away(k).wait_send()
            far(k).wait_send()

        return carry

    lax.fori_loop(1, pairs, drain, 0)


def local(out_grad, expert_index, gate_values, dispatched_inputs, w_gate, w_up, w_down):
    sources = lax.axis_size("expert")
    pairs = sources // 2
    tokens, width = out_grad.shape
    units = w_gate.shape[2]
    share = width // lax.axis_size("hidden")
    lanes = (share + 128) // 128 * 128
    capacity = 2 * dispatched_inputs.shape[1] // sources
    start = capacity // 16 * 16
    capp = (2 * capacity - start + 15) // 16 * 16
    sent = (2 * capacity - start + 7) // 8 * 8
    rows_all = start + capp
    assert sent <= 128
    fold = 0 if share % 128 == 0 else (sent + 15) // 16 * 8 if share % 128 == 64 else sent
    packed = share // 128 * sent + fold + 8
    wide = (share + 127) // 128 * 128
    own = dispatched_inputs[0]
    saved_rows = 2 * capacity
    if saved_rows % 8:
        own = jnp.pad(
            own.reshape(pairs // 2, saved_rows, width),
            ((0, 0), (0, rows_all - saved_rows), (0, 0)),
        ).reshape(-1, width)
        saved_rows = rows_all
    bf16, f32 = jnp.bfloat16, jnp.float32
    vmem = pl.BlockSpec(memory_space=pltpu.VMEM)
    hbm = pl.BlockSpec(memory_space=pl.ANY)
    dma = pltpu.SemaphoreType.DMA
    input_grad, gate_grad = pl.pallas_call(
        functools.partial(kernel, pairs, capacity, start, capp, sent, saved_rows, share, lanes),
        out_shape=(
            pltpu.VMEM((tokens, share), bf16),
            pltpu.VMEM((2, tokens), bf16),
        ),
        in_specs=[hbm] * 7,
        out_specs=(vmem, vmem),
        scratch_shapes=[
            pltpu.VMEM((2, tokens), jnp.int32),
            pltpu.VMEM((2, tokens), f32),
            pltpu.VMEM((tokens, width), bf16),
            pltpu.VMEM((max(16, pairs), tokens), jnp.int32),
            pltpu.VMEM((pairs, 2 * tokens, sent), bf16),
            pltpu.VMEM((tokens, wide), f32),
            pltpu.VMEM((2, tokens), f32),
            pltpu.VMEM((pairs, capp, width), bf16),
            pltpu.VMEM((width, units), bf16),
            pltpu.VMEM((width, units), bf16),
            pltpu.VMEM((units, width), bf16),
            pltpu.VMEM((2 * lanes, units), bf16),
            pltpu.VMEM((2 * lanes, units), bf16),
            pltpu.VMEM((pairs, rows_all, width), bf16),
            pltpu.VMEM((sources, capp, width), bf16),
            pltpu.VMEM((pairs, rows_all, units), f32),
            pltpu.VMEM((pairs, rows_all, units), f32),
            pltpu.VMEM((pairs, rows_all, units), f32),
            pltpu.VMEM((2, 2, 2, packed, 128), f32),
            pltpu.VMEM((pairs, packed, 128), f32),
            pltpu.VMEM((pairs, 2, packed, 128), bf16),
            pltpu.VMEM((pairs, 2, packed, 128), bf16),
            pltpu.VMEM((pairs, packed, 128), bf16),
            pltpu.VMEM((pairs, packed, 128), bf16),
            pltpu.VMEM((pairs, packed, 128), bf16),
            pltpu.VMEM((pairs, packed, 128), bf16),
            dma((3,)),
            dma((7,)),
            dma((pairs // 2,)),
            dma((pairs // 2,)),
            dma((pairs // 2,)),
            dma((pairs,)),
            dma((sources,)),
            dma((pairs,)),
            dma((pairs,)),
            dma((pairs,)),
            dma((pairs,)),
            dma((pairs,)),
            dma((pairs,)),
            dma((pairs,)),
            dma((pairs,)),
        ],
        compiler_params=pltpu.CompilerParams(
            collective_id=0, has_side_effects=True, vmem_limit_bytes=60 * 1024 * 1024
        ),
    )(expert_index.T, gate_values.T, out_grad, own, w_gate[0], w_up[0], w_down[0])
    return input_grad, gate_grad.T


def solution(mesh):
    in_specs = (
        P(("groups", "expert", "tok"), None),
        P(("groups", "expert", "tok"), None),
        P(("groups", "expert", "tok"), None),
        P("expert", ("groups", "tok"), None),
        P("expert", None, "hidden"),
        P("expert", None, "hidden"),
        P("expert", "hidden", None),
    )
    out_specs = (P(("groups", "expert", "tok"), "hidden"), P(("groups", "expert", "tok"), None))
    return jax.shard_map(local, mesh=mesh, in_specs=in_specs, out_specs=out_specs, check_vma=False)
```
